256 devices in a mesh: samp: 32 (over x, z), reg: 8 (over y, core).
Axes of the slice: x: 4, y: 4, z: 8, core: 2. Of those that a mesh axis runs over, the one named last changes fastest.
Arguments:
- library: bfloat16 [98304, 1024], P('samp'), as said below
- responses: bfloat16 [98304, 1024], P('samp', 'reg'), as said below
- coefficients: float32 [1024, 1024], P(None, 'reg'), as said below
Outputs:
- updated: float32 [1024, 1024], P(None, 'reg')
Inputs may be any that keep to these rules, and one draw needn't show every extreme that they name: library entries are finite; column and row scales differ. responses are finite. coefficients are finite.
All inputs are finite; a program needn't handle non-finite values.
Results may differ from the reference program's by a relative error of at most 0.0041.
Values sent between devices are 32-bit elements; how exact they have to be, the bound alone decides.
No kernel may reach another device: no remote copies, remote signals or barrier semaphores. Data moves between devices by JAX's collectives and lax.ppermute only.
A program may use at most 64 MiB of HBM per device.

```python
import math
import jax
import jax.numpy as jnp
from jax import lax

P_SIZE = 1024
R = 1024
ITERS = 2
S = 98304


def draw_library(key, part):
    position = jnp.arange(S, dtype=jnp.float32) / max(S - 1, 1)
    rising = 1.0 + 2.0 * position
    column_scale = jnp.exp(jax.random.uniform(jax.random.fold_in(key, 2), (P_SIZE,), jnp.float32, 0.0, math.log(10.0)))
    base = jnp.clip(jax.random.normal(jax.random.fold_in(key, 1), (S, P_SIZE), jnp.float32), -6.0, 6.0)
    return (base * rising[:, None] * column_scale[None, :]).astype(jnp.bfloat16)


def draw_responses(key, part):
    column_scale = 16.0 * jnp.exp(jax.random.uniform(jax.random.fold_in(key, 5), (R,), jnp.float32, 0.0, math.log(10.0)))
    base = jnp.clip(jax.random.normal(jax.random.fold_in(key, 4), (S, R), jnp.float32), -6.0, 6.0)
    return (base * column_scale[None, :]).astype(jnp.bfloat16)


def draw_coefficients(key, part):
    row_scale = jnp.exp(jax.random.uniform(jax.random.fold_in(key, 7), (P_SIZE,), jnp.float32, math.log(0.1), 0.0))
    column_scale = jnp.exp(jax.random.uniform(jax.random.fold_in(key, 8), (R,), jnp.float32, math.log(0.3), math.log(3.0)))
    base = jnp.clip(jax.random.normal(jax.random.fold_in(key, 6), (P_SIZE, R), jnp.float32), -6.0, 6.0)
    return base * row_scale[:, None] * column_scale[None, :]


def setup_inputs(seed: int = 0) -> dict:
    key_list = jax.random.split(jax.random.key(seed), 4)
    return {
        "library": draw_library(jax.random.fold_in(key_list[3], 71), 0),
        "responses": draw_responses(jax.random.fold_in(key_list[3], 71), 0),
        "coefficients": draw_coefficients(jax.random.fold_in(key_list[3], 71), 0),
    }


STEP_SCALE = 0.5
PENALTY = 40.0
EPSILON = 1e-06

def reference(library, responses, coefficients):
    column_sq = lax.optimization_barrier(jnp.sum(jnp.square(library.astype(jnp.float32)), axis=0))
    step_sizes = STEP_SCALE * S / column_sq
    moved = coefficients
    for turn in range(ITERS):
        weights_bf = moved.astype(jnp.bfloat16)
        residual = (jnp.dot(library, weights_bf, preferred_element_type=jnp.float32) - responses.astype(jnp.float32)).astype(jnp.bfloat16)
        gradient = lax.dot_general(library, residual, (((0,), (0,)), ((), ())), preferred_element_type=jnp.float32) / S
        trial = moved - step_sizes[:, None] * gradient
        norms = jnp.sqrt(lax.optimization_barrier(jnp.sum(trial * trial, axis=1)) + EPSILON)
        factor = jnp.maximum(0.0, 1.0 - PENALTY * step_sizes / norms)
        moved = trial * factor[:, None]
    return moved
```

```python
import jax
import jax.numpy as jnp
from jax import lax
from jax.experimental import pallas as pl
from jax.experimental.pallas import tpu as pltpu
from jax.sharding import PartitionSpec as P

STEP_SCALE = 0.5
PENALTY = 40.0
EPSILON = 1e-06
LANES = 128
F32 = jnp.float32
BF16 = jnp.bfloat16
VMEM_LIMIT = 48 << 20


def params():
    return pltpu.CompilerParams(vmem_limit_bytes=VMEM_LIMIT)


def to_column(row, first, rows):
    lane = lax.broadcasted_iota(jnp.int32, (rows, LANES), 1)
    own = lax.broadcasted_iota(jnp.int32, (rows, LANES), 0) + first
    return jnp.sum(jnp.where(lane == own, row, 0.0), axis=1, keepdims=True)


def to_row(column):
    rows = column.shape[0]
    lane = lax.broadcasted_iota(jnp.int32, (rows, LANES), 1)
    own = lax.broadcasted_iota(jnp.int32, (rows, LANES), 0)
    return jnp.sum(jnp.where(lane == own, column, 0.0), axis=0, keepdims=True)


def correlate_kernel(place, lib, lib_cols, resp, coef, out, acc, squares):
    step, last = pl.program_id(0), pl.num_programs(0) - 1
    block = lib[...]
    residual = (
        jnp.dot(block, coef[...].astype(BF16), preferred_element_type=F32)
        - resp[...].astype(F32)
    ).astype(BF16)
    right = jnp.concatenate([residual, lib_cols[...]], axis=1)
    part = lax.dot_general(block, right, (((0,), (0,)), ((), ())), preferred_element_type=F32)
    wide = block.astype(F32)
    part_sq = jnp.sum((wide * wide).reshape(-1, 8, wide.shape[1]), axis=0)

    @pl.when(step == 0)
    def _():
        acc[...] = part
        squares[...] = part_sq

    @pl.when(step > 0)
    def _():
        acc[...] += part
        squares[...] += part_sq

    @pl.when(step == last)
    def _():
        chunks = 32
        rows = acc.shape[0] // chunks
        tall = 2 * rows + 1
        column_sq = jnp.sum(squares[...], axis=0, keepdims=True)
        for c in range(chunks):
            out[c * tall:c * tall + rows, :] = acc[c * rows:(c + 1) * rows, :LANES]
            out[c * tall + rows:c * tall + 2 * rows, :] = acc[c * rows:(c + 1) * rows, LANES:]
            at = c * rows // LANES * LANES
            out[c * tall + 2 * rows:(c + 1) * tall, :] = column_sq[:, at:at + LANES]


def correlate(place, library, responses, coefficients, block=512):
    samples, terms = library.shape
    return pl.pallas_call(
        correlate_kernel,
        out_shape=jax.ShapeDtypeStruct((2 * terms + 32, LANES), F32),
        grid_spec=pltpu.PrefetchScalarGridSpec(
            num_scalar_prefetch=1,
            grid=(samples // block,),
            in_specs=[
                pl.BlockSpec((block, terms), lambda i, place: (i, 0)),
                pl.BlockSpec((block, LANES), lambda i, place: (i, place[1])),
                pl.BlockSpec((block, LANES), lambda i, place: (i, 0)),
                pl.BlockSpec((terms, LANES), lambda i, place: (0, 0)),
            ],
            out_specs=pl.BlockSpec((2 * terms + 32, LANES), lambda i, place: (0, 0)),
            scratch_shapes=[
                pltpu.VMEM((terms, 2 * LANES), F32),
                pltpu.VMEM((8, terms), F32),
            ],
        ),
        compiler_params=params(),
        name="correlate",
    )(place, library, library, responses, coefficients)


def first_step_kernel(place, parts, coef, send, state, *, rows, samples):
    tall = 2 * rows + 1
    total = parts[0:2 * rows, :]
    column_sq = parts[2 * rows:tall, :]
    for c in range(1, parts.shape[0] // tall):
        total += parts[c * tall:c * tall + 2 * rows, :]
        column_sq += parts[c * tall + 2 * rows:(c + 1) * tall, :]
    step = STEP_SCALE * samples / to_column(column_sq, place[0] * rows % LANES, rows)
    corr, gram = total[:rows], total[rows:]
    trial = coef[...] - step * (corr / samples)
    squares = to_row(jnp.sum(trial * trial, axis=1, keepdims=True))
    for c in range(8):
        send[c * (rows + 1):c * (rows + 1) + rows, :] = gram
        send[c * (rows + 1) + rows:(c + 1) * (rows + 1), :] = squares
    state[0:rows, :] = trial
    state[rows:2 * rows, :] = corr
    state[2 * rows:3 * rows, :] = jnp.broadcast_to(step, (rows, LANES))


def shrink(trial, squares, step):
    norms = jnp.sqrt(squares + EPSILON)
    return trial * jnp.maximum(0.0, 1.0 - PENALTY * step / norms)


def first_shrink_kernel(gathered, state, moved, *, rows):
    squares = gathered[rows:rows + 1, :]
    for c in range(1, 8):
        squares += gathered[c * (rows + 1) + rows:(c + 1) * (rows + 1), :]
    own = shrink(state[0:rows, :], to_column(squares, 0, rows), state[2 * rows:3 * rows, :])
    for c in range(32):
        moved[c * rows:(c + 1) * rows, :] = own


def second_step_kernel(moved, coef, gathered, state, own, send, trial_out, *, rows, samples):
    change = moved[...].astype(BF16).astype(F32) - coef[...].astype(BF16).astype(F32)
    corr = state[rows:2 * rows, :]
    for c in range(8):
        corr += jnp.dot(
            gathered[c * (rows + 1):c * (rows + 1) + rows, :],
            change[c * LANES:(c + 1) * LANES, :],
            precision=lax.Precision.HIGHEST,
            preferred_element_type=F32,
        )
    trial = own[...] - state[2 * rows:3 * rows, :] * (corr / samples)
    squares = to_row(jnp.sum(trial * trial, axis=1, keepdims=True))
    send[...] = jnp.broadcast_to(squares, (8, LANES))
    trial_out[...] = trial


def second_shrink_kernel(squares, trial, state, moved, *, rows):
    total = jnp.sum(squares[...], axis=0, keepdims=True)
    own = shrink(trial[...], to_column(total, 0, rows), state[2 * rows:3 * rows, :])
    for c in range(32):
        moved[c * rows:(c + 1) * rows, :] = own


def whole(kernel, name, out_shapes, *arrays, **fixed):
    return pl.pallas_call(
        lambda *refs: kernel(*refs, **fixed),
        out_shape=[jax.ShapeDtypeStruct(s, F32) for s in out_shapes],
        compiler_params=params(),
        name=name,
    )(*arrays)


def exchange(array, axis, count):
    blocks = array.reshape(count, array.shape[0] // count, 1, LANES)
    return lax.all_to_all(blocks, axis, 0, 0).reshape(array.shape)


def shards(library, responses, coefficients):
    n_samp, n_reg = lax.axis_size("samp"), lax.axis_size("reg")
    samples, terms = library.shape[0] * n_samp, library.shape[1]
    rows = terms // n_samp
    place = jnp.stack([lax.axis_index("samp"), lax.axis_index("reg")]).astype(jnp.int32)

    parts = correlate(place, library, responses, coefficients)
    parts = exchange(parts, "samp", n_samp)

    send, state = pl.pallas_call(
        lambda *refs: first_step_kernel(*refs, rows=rows, samples=samples),
        out_shape=[
            jax.ShapeDtypeStruct((n_reg * (rows + 1), LANES), F32),
            jax.ShapeDtypeStruct((3 * rows, LANES), F32),
        ],
        grid_spec=pltpu.PrefetchScalarGridSpec(
            num_scalar_prefetch=1,
            grid=(1,),
            in_specs=[
                pl.BlockSpec(parts.shape, lambda i, place: (0, 0)),
                pl.BlockSpec((rows, LANES), lambda i, place: (place[0], 0)),
            ],
            out_specs=[
                pl.BlockSpec((n_reg * (rows + 1), LANES), lambda i, place: (0, 0)),
                pl.BlockSpec((3 * rows, LANES), lambda i, place: (0, 0)),
            ],
        ),
        compiler_params=params(),
        name="first_step",
    )(place, parts, coefficients)
    gathered = exchange(send, "reg", n_reg)

    (spread,) = whole(first_shrink_kernel, "first_shrink", [(terms, LANES)], gathered, state, rows=rows)
    own = spread[:rows]
    moved = exchange(spread, "samp", n_samp)

    send, trial = whole(
        second_step_kernel, "second_step", [(n_reg, LANES), (rows, LANES)],
        moved, coefficients, gathered, state, own, rows=rows, samples=samples,
    )
    squares = exchange(send, "reg", n_reg)
    (spread,) = whole(
        second_shrink_kernel, "second_shrink", [(terms, LANES)], squares, trial, state, rows=rows
    )
    return exchange(spread, "samp", n_samp)


def solution(mesh):
    return jax.shard_map(
        shards,
        mesh=mesh,
        in_specs=(P("samp", None), P("samp", "reg"), P(None, "reg")),
        out_specs=P(None, "reg"),
        check_vma=False,
    )
```

```python
import jax
import jax.numpy as jnp
from jax import lax
from jax.experimental import pallas as pl
from jax.experimental.pallas import tpu as pltpu
from jax.sharding import PartitionSpec as P

STEP_SCALE = 0.5
PENALTY = 40.0
EPSILON = 1e-06
LANES = 128
F32 = jnp.float32
BF16 = jnp.bfloat16
VMEM_LIMIT = 48 << 20
AHEAD = 2
N_X = 4


def params():
    return pltpu.CompilerParams(vmem_limit_bytes=VMEM_LIMIT)


def to_column(row, first, rows):
    lane = lax.broadcasted_iota(jnp.int32, (rows, LANES), 1)
    own = lax.broadcasted_iota(jnp.int32, (rows, LANES), 0) + first
    return jnp.sum(jnp.where(lane == own, row, 0.0), axis=1, keepdims=True)


def to_row(column):
    rows = column.shape[0]
    lane = lax.broadcasted_iota(jnp.int32, (rows, LANES), 1)
    own = lax.broadcasted_iota(jnp.int32, (rows, LANES), 0)
    return jnp.sum(jnp.where(lane == own, column, 0.0), axis=0, keepdims=True)


def correlate_kernel(place, lib_hbm, resp_hbm, coef_hbm, out, lib, resp, coef, acc, squares, sems, *, blocks, chunks):
    count = len(blocks)
    starts = [sum(blocks[:i]) for i in range(count)]
    copies = [
        pltpu.make_async_copy(lib_hbm.at[pl.ds(at, size)], lib.at[pl.ds(at, size)], sems.at[i])
        for i, (at, size) in enumerate(zip(starts, blocks))
    ]
    copy_coef = pltpu.make_async_copy(coef_hbm, coef, sems.at[count])
    copy_resp = pltpu.make_async_copy(resp_hbm, resp, sems.at[count + 1])
    copy_coef.start()
    for i in range(AHEAD):
        copies[i].start()
    copy_resp.start()
    copy_coef.wait()
    weights = coef[...].astype(BF16)
    own = pl.multiple_of(place[1] * LANES, LANES)
    residuals = {}

    def residual(i):
        copies[i].wait()
        if i + AHEAD < count:
            copies[i + AHEAD].start()
        if i == 0:
            copy_resp.wait()
        at = pl.ds(starts[i], blocks[i])
        fit = jnp.dot(lib[at, :], weights, preferred_element_type=F32)
        residuals[i] = (fit - resp[at, :].astype(F32)).astype(BF16)

    def correlation(i):
        at = pl.ds(starts[i], blocks[i])
        block = lib[at, :]
        right = jnp.concatenate([residuals[i], lib[at, pl.ds(own, LANES)]], axis=1)
        part = lax.dot_general(block, right, (((0,), (0,)), ((), ())), preferred_element_type=F32)
        wide = block.astype(F32)
        part_sq = jnp.sum((wide * wide).reshape(-1, 8, wide.shape[1]), axis=0)
        if i == 0:
            acc[...] = part
            squares[...] = part_sq
        else:
            acc[...] += part
            squares[...] += part_sq

    for i in range(count):
        residual(i)
        if i > 0:
            correlation(i - 1)
    correlation(count - 1)

    rows = acc.shape[0] // chunks
    tall = 2 * rows + 1
    column_sq = jnp.sum(squares[...], axis=0, keepdims=True)
    for c in range(chunks):
        out[c * tall:c * tall + rows, :] = acc[c * rows:(c + 1) * rows, :LANES]
        out[c * tall + rows:c * tall + 2 * rows, :] = acc[c * rows:(c + 1) * rows, LANES:]
        at = c * rows // LANES * LANES
        out[c * tall + 2 * rows:(c + 1) * tall, :] = column_sq[:, at:at + LANES]


def block_sizes(samples):
    unit = samples // 12
    return (unit, unit, 2 * unit, 4 * unit, 4 * unit)


def correlate(place, library, responses, coefficients, chunks):
    samples, terms = library.shape
    blocks = block_sizes(samples)
    hbm = pl.BlockSpec(memory_space=pltpu.HBM)
    return pl.pallas_call(
        lambda *refs: correlate_kernel(*refs, blocks=blocks, chunks=chunks),
        out_shape=jax.ShapeDtypeStruct((2 * terms + chunks, LANES), F32),
        in_specs=[pl.BlockSpec(memory_space=pltpu.SMEM), hbm, hbm, hbm],
        scratch_shapes=[
            pltpu.VMEM((samples, terms), BF16),
            pltpu.VMEM((samples, LANES), BF16),
            pltpu.VMEM((terms, LANES), F32),
            pltpu.VMEM((terms, 2 * LANES), F32),
            pltpu.VMEM((8, terms), F32),
            pltpu.SemaphoreType.DMA((len(blocks) + 2,)),
        ],
        compiler_params=params(),
        name="correlate",
    )(place, library, responses, coefficients)


def add_kernel(parts, out):
    tall = out.shape[0]
    total = parts[0:tall, :]
    for c in range(1, parts.shape[0] // tall):
        total += parts[c * tall:(c + 1) * tall, :]
    out[...] = total


def first_step_kernel(place, parts, coef, send, state, *, rows, samples):
    tall = 2 * rows + 1
    total = parts[0:2 * rows, :]
    column_sq = parts[2 * rows:tall, :]
    for c in range(1, parts.shape[0] // tall):
        total += parts[c * tall:c * tall + 2 * rows, :]
        column_sq += parts[c * tall + 2 * rows:(c + 1) * tall, :]
    step = STEP_SCALE * samples / to_column(column_sq, place[0] * rows % LANES, rows)
    corr, gram = total[:rows], total[rows:]
    trial = coef[...] - step * (corr / samples)
    squares = to_row(jnp.sum(trial * trial, axis=1, keepdims=True))
    for c in range(8):
        send[c * (rows + 1):c * (rows + 1) + rows, :] = gram
        send[c * (rows + 1) + rows:(c + 1) * (rows + 1), :] = squares
    state[0:rows, :] = trial
    state[rows:2 * rows, :] = corr
    state[2 * rows:3 * rows, :] = jnp.broadcast_to(step, (rows, LANES))


def shrink(trial, squares, step):
    norms = jnp.sqrt(squares + EPSILON)
    return trial * jnp.maximum(0.0, 1.0 - PENALTY * step / norms)


def first_shrink_kernel(gathered, state, moved, own_out, *, rows):
    squares = gathered[rows:rows + 1, :]
    for c in range(1, 8):
        squares += gathered[c * (rows + 1) + rows:(c + 1) * (rows + 1), :]
    own = shrink(state[0:rows, :], to_column(squares, 0, rows), state[2 * rows:3 * rows, :])
    own_out[...] = own
    for c in range(32):
        moved[c * rows:(c + 1) * rows, :] = own


def second_step_kernel(moved, coef, gathered, state, own, send, trial_out, *, rows, samples):
    change = moved[...].astype(BF16).astype(F32) - coef[...].astype(BF16).astype(F32)
    corr = state[rows:2 * rows, :]
    for c in range(8):
        corr += jnp.dot(
            gathered[c * (rows + 1):c * (rows + 1) + rows, :],
            change[c * LANES:(c + 1) * LANES, :],
            precision=lax.Precision.HIGHEST,
            preferred_element_type=F32,
        )
    trial = own[...] - state[2 * rows:3 * rows, :] * (corr / samples)
    squares = to_row(jnp.sum(trial * trial, axis=1, keepdims=True))
    send[...] = jnp.broadcast_to(squares, (8, LANES))
    trial_out[...] = trial


def second_shrink_kernel(squares, trial, state, moved, *, rows):
    total = jnp.sum(squares[...], axis=0, keepdims=True)
    own = shrink(trial[...], to_column(total, 0, rows), state[2 * rows:3 * rows, :])
    for c in range(32):
        moved[c * rows:(c + 1) * rows, :] = own


def whole(kernel, name, out_shapes, *arrays, **fixed):
    return pl.pallas_call(
        lambda *refs: kernel(*refs, **fixed),
        out_shape=[jax.ShapeDtypeStruct(s, F32) for s in out_shapes],
        compiler_params=params(),
        name=name,
    )(*arrays)


def exchange(array, axis, count, groups=None):
    blocks = array.reshape(count, array.shape[0] // count, 1, LANES)
    return lax.all_to_all(blocks, axis, 0, 0, axis_index_groups=groups).reshape(array.shape)


def shards(library, responses, coefficients):
    n_samp, n_reg = lax.axis_size("samp"), lax.axis_size("reg")
    samples, terms = library.shape[0] * n_samp, library.shape[1]
    rows = terms // n_samp
    place = jnp.stack([lax.axis_index("samp"), lax.axis_index("reg")]).astype(jnp.int32)

    n_z = n_samp // N_X
    over_x = [[x * n_z + z for x in range(N_X)] for z in range(n_z)]
    over_z = [[x * n_z + z for z in range(n_z)] for x in range(N_X)]
    parts = correlate(place, library, responses, coefficients, n_samp)
    parts = exchange(parts, "samp", N_X, over_x)
    (parts,) = whole(add_kernel, "add", [(parts.shape[0] // N_X, LANES)], parts)
    parts = exchange(parts, "samp", n_z, over_z)

    send, state = pl.pallas_call(
        lambda *refs: first_step_kernel(*refs, rows=rows, samples=samples),
        out_shape=[
            jax.ShapeDtypeStruct((n_reg * (rows + 1), LANES), F32),
            jax.ShapeDtypeStruct((3 * rows, LANES), F32),
        ],
        grid_spec=pltpu.PrefetchScalarGridSpec(
            num_scalar_prefetch=1,
            grid=(1,),
            in_specs=[
                pl.BlockSpec(parts.shape, lambda i, place: (0, 0)),
                pl.BlockSpec((rows, LANES), lambda i, place: (place[0], 0)),
            ],
            out_specs=[
                pl.BlockSpec((n_reg * (rows + 1), LANES), lambda i, place: (0, 0)),
                pl.BlockSpec((3 * rows, LANES), lambda i, place: (0, 0)),
            ],
        ),
        compiler_params=params(),
        name="first_step",
    )(place, parts, coefficients)
    gathered = exchange(send, "reg", n_reg)

    spread, own = whole(
        first_shrink_kernel, "first_shrink", [(terms, LANES), (rows, LANES)], gathered, state, rows=rows
    )
    moved = exchange(spread, "samp", n_samp)

    send, trial = whole(
        second_step_kernel, "second_step", [(n_reg, LANES), (rows, LANES)],
        moved, coefficients, gathered, state, own, rows=rows, samples=samples,
    )
    squares = exchange(send, "reg", n_reg)
    (spread,) = whole(
        second_shrink_kernel, "second_shrink", [(terms, LANES)], squares, trial, state, rows=rows
    )
    return exchange(spread, "samp", n_samp)


def solution(mesh):
    return jax.shard_map(
        shards,
        mesh=mesh,
        in_specs=(P("samp", None), P("samp", "reg"), P(None, "reg")),
        out_specs=P(None, "reg"),
        check_vma=False,
    )
```

```python
import jax
import jax.numpy as jnp
from jax import lax
from jax.experimental import pallas as pl
from jax.experimental.pallas import tpu as pltpu
from jax.sharding import PartitionSpec as P

STEP_SCALE = 0.5
PENALTY = 40.0
EPSILON = 1e-06
LANES = 128
F32 = jnp.float32
BF16 = jnp.bfloat16
VMEM_LIMIT = 48 << 20
AHEAD = 2
N_X = 4


def params():
    return pltpu.CompilerParams(vmem_limit_bytes=VMEM_LIMIT)


def to_column(row, first, rows):
    lane = lax.broadcasted_iota(jnp.int32, (rows, LANES), 1)
    own = lax.broadcasted_iota(jnp.int32, (rows, LANES), 0) + first
    return jnp.sum(jnp.where(lane == own, row, 0.0), axis=1, keepdims=True)


def to_row(column):
    rows = column.shape[0]
    lane = lax.broadcasted_iota(jnp.int32, (rows, LANES), 1)
    own = lax.broadcasted_iota(jnp.int32, (rows, LANES), 0)
    return jnp.sum(jnp.where(lane == own, column, 0.0), axis=0, keepdims=True)


def correlate_kernel(place, lib_hbm, resp_hbm, coef_hbm, out, lib, resp, coef, acc, squares, sems, *, blocks, chunks):
    count = len(blocks)
    starts = [sum(blocks[:i]) for i in range(count)]
    copies = [
        pltpu.make_async_copy(lib_hbm.at[pl.ds(at, size)], lib.at[pl.ds(at, size)], sems.at[i])
        for i, (at, size) in enumerate(zip(starts, blocks))
    ]
    copy_coef = pltpu.make_async_copy(coef_hbm, coef, sems.at[count])
    copy_resp = pltpu.make_async_copy(resp_hbm, resp, sems.at[count + 1])
    copy_coef.start()
    for i in range(AHEAD):
        copies[i].start()
    copy_resp.start()
    copy_coef.wait()
    weights = coef[...].astype(BF16)
    own = pl.multiple_of(place[1] * LANES, LANES)
    residuals = {}

    def residual(i):
        copies[i].wait()
        if i + AHEAD < count:
            copies[i + AHEAD].start()
        if i == 0:
            copy_resp.wait()
        at = pl.ds(starts[i], blocks[i])
        fit = jnp.dot(lib[at, :], weights, preferred_element_type=F32)
        residuals[i] = (fit - resp[at, :].astype(F32)).astype(BF16)

    def correlation(i):
        at = pl.ds(starts[i], blocks[i])
        block = lib[at, :]
        right = jnp.concatenate([residuals[i], lib[at, pl.ds(own, LANES)]], axis=1)
        part = lax.dot_general(block, right, (((0,), (0,)), ((), ())), preferred_element_type=F32)
        wide = block.astype(F32)
        part_sq = jnp.sum((wide * wide).reshape(-1, 8, wide.shape[1]), axis=0)
        if i == 0:
            acc[...] = part
            squares[...] = part_sq
        else:
            acc[...] += part
            squares[...] += part_sq

    for i in range(count):
        residual(i)
        if i > 0:
            correlation(i - 1)
    correlation(count - 1)

    rows = acc.shape[0] // chunks
    tall = 2 * rows + 1
    column_sq = jnp.sum(squares[...], axis=0, keepdims=True)
    for c in range(chunks):
        out[c * tall:c * tall + rows, :] = acc[c * rows:(c + 1) * rows, :LANES]
        out[c * tall + rows:c * tall + 2 * rows, :] = acc[c * rows:(c + 1) * rows, LANES:]
        at = c * rows // LANES * LANES
        out[c * tall + 2 * rows:(c + 1) * tall, :] = column_sq[:, at:at + LANES]


def block_sizes(samples):
    unit = samples // 12
    return (unit, unit, 2 * unit, 4 * unit, 4 * unit)


def correlate(place, library, responses, coefficients, chunks):
    samples, terms = library.shape
    blocks = block_sizes(samples)
    hbm = pl.BlockSpec(memory_space=pltpu.HBM)
    return pl.pallas_call(
        lambda *refs: correlate_kernel(*refs, blocks=blocks, chunks=chunks),
        out_shape=jax.ShapeDtypeStruct((2 * terms + chunks, LANES), F32),
        in_specs=[pl.BlockSpec(memory_space=pltpu.SMEM), hbm, hbm, hbm],
        scratch_shapes=[
            pltpu.VMEM((samples, terms), BF16),
            pltpu.VMEM((samples, LANES), BF16),
            pltpu.VMEM((terms, LANES), F32),
            pltpu.VMEM((terms, 2 * LANES), F32),
            pltpu.VMEM((8, terms), F32),
            pltpu.SemaphoreType.DMA((len(blocks) + 2,)),
        ],
        compiler_params=params(),
        name="correlate",
    )(place, library, *(pltpu.with_memory_space_constraint(a, pltpu.HBM) for a in (responses, coefficients)))


def add_kernel(parts, out):
    tall = out.shape[0]
    total = parts[0:tall, :]
    for c in range(1, parts.shape[0] // tall):
        total += parts[c * tall:(c + 1) * tall, :]
    out[...] = total


def first_step_kernel(place, parts, coef, send, gram_out, state, *, rows, samples):
    tall = 2 * rows + 1
    total = parts[0:2 * rows, :]
    column_sq = parts[2 * rows:tall, :]
    for c in range(1, parts.shape[0] // tall):
        total += parts[c * tall:c * tall + 2 * rows, :]
        column_sq += parts[c * tall + 2 * rows:(c + 1) * tall, :]
    step = STEP_SCALE * samples / to_column(column_sq, place[0] * rows % LANES, rows)
    corr, gram = total[:rows], total[rows:]
    trial = coef[...] - step * (corr / samples)
    squares = to_row(jnp.sum(trial * trial, axis=1, keepdims=True))
    send[...] = jnp.broadcast_to(squares, send.shape)
    gram_out[...] = gram
    state[0:rows, :] = trial
    state[rows:2 * rows, :] = corr
    state[2 * rows:3 * rows, :] = jnp.broadcast_to(step, (rows, LANES))


def shrink(trial, squares, step):
    norms = jnp.sqrt(squares + EPSILON)
    return trial * jnp.maximum(0.0, 1.0 - PENALTY * step / norms)


def first_shrink_kernel(squares, state, moved, own_out, *, rows):
    total = jnp.sum(squares[...], axis=0, keepdims=True)
    own = shrink(state[0:rows, :], to_column(total, 0, rows), state[2 * rows:3 * rows, :])
    own_out[...] = own
    for c in range(32):
        moved[c * rows:(c + 1) * rows, :] = own


def second_step_kernel(moved, coef, gram, state, own, send, trial_out, *, rows, samples):
    change = moved[...].astype(BF16).astype(F32) - coef[...].astype(BF16).astype(F32)
    corr = state[rows:2 * rows, :]
    for c in range(8):
        corr += jnp.dot(
            gram[c * rows:(c + 1) * rows, :],
            change[c * LANES:(c + 1) * LANES, :],
            precision=lax.Precision.HIGHEST,
            preferred_element_type=F32,
        )
    trial = own[...] - state[2 * rows:3 * rows, :] * (corr / samples)
    squares = to_row(jnp.sum(trial * trial, axis=1, keepdims=True))
    send[...] = jnp.broadcast_to(squares, (8, LANES))
    trial_out[...] = trial


def second_shrink_kernel(squares, trial, state, moved, *, rows):
    total = jnp.sum(squares[...], axis=0, keepdims=True)
    own = shrink(trial[...], to_column(total, 0, rows), state[2 * rows:3 * rows, :])
    for c in range(32):
        moved[c * rows:(c + 1) * rows, :] = own


def whole(kernel, name, out_shapes, *arrays, **fixed):
    return pl.pallas_call(
        lambda *refs: kernel(*refs, **fixed),
        out_shape=[jax.ShapeDtypeStruct(s, F32) for s in out_shapes],
        compiler_params=params(),
        name=name,
    )(*arrays)


def exchange(array, axis, count, groups=None):
    blocks = array.reshape(count, array.shape[0] // count, 1, LANES)
    return lax.all_to_all(blocks, axis, 0, 0, axis_index_groups=groups).reshape(array.shape)


def shards(library, responses, coefficients):
    n_samp, n_reg = lax.axis_size("samp"), lax.axis_size("reg")
    samples, terms = library.shape[0] * n_samp, library.shape[1]
    rows = terms // n_samp
    place = jnp.stack([lax.axis_index("samp"), lax.axis_index("reg")]).astype(jnp.int32)

    n_z = n_samp // N_X
    over_x = [[x * n_z + z for x in range(N_X)] for z in range(n_z)]
    over_z = [[x * n_z + z for z in range(n_z)] for x in range(N_X)]
    parts = correlate(place, library, responses, coefficients, n_samp)
    parts = exchange(parts, "samp", N_X, over_x)
    (parts,) = whole(add_kernel, "add", [(parts.shape[0] // N_X, LANES)], parts)
    parts = exchange(parts, "samp", n_z, over_z)

    send, gram, state = pl.pallas_call(
        lambda *refs: first_step_kernel(*refs, rows=rows, samples=samples),
        out_shape=[
            jax.ShapeDtypeStruct((n_reg, LANES), F32),
            jax.ShapeDtypeStruct((rows, LANES), F32),
            jax.ShapeDtypeStruct((3 * rows, LANES), F32),
        ],
        grid_spec=pltpu.PrefetchScalarGridSpec(
            num_scalar_prefetch=1,
            grid=(1,),
            in_specs=[
                pl.BlockSpec(parts.shape, lambda i, place: (0, 0)),
                pl.BlockSpec((rows, LANES), lambda i, place: (place[0], 0)),
            ],
            out_specs=[
                pl.BlockSpec((n_reg, LANES), lambda i, place: (0, 0)),
                pl.BlockSpec((rows, LANES), lambda i, place: (0, 0)),
                pl.BlockSpec((3 * rows, LANES), lambda i, place: (0, 0)),
            ],
        ),
        compiler_params=params(),
        name="first_step",
    )(place, parts, coefficients)
    squares = exchange(send, "reg", n_reg)
    spread, own = whole(
        first_shrink_kernel, "first_shrink", [(terms, LANES), (rows, LANES)], squares, state, rows=rows
    )
    gram = lax.all_gather(gram, "reg", axis=0, tiled=True)
    moved = exchange(spread, "samp", n_samp)

    send, trial = whole(
        second_step_kernel, "second_step", [(n_reg, LANES), (rows, LANES)],
        moved, coefficients, gram, state, own, rows=rows, samples=samples,
    )
    squares = exchange(send, "reg", n_reg)
    (spread,) = whole(
        second_shrink_kernel, "second_shrink", [(terms, LANES)], squares, trial, state, rows=rows
    )
    return exchange(spread, "samp", n_samp)


def solution(mesh):
    return jax.shard_map(
        shards,
        mesh=mesh,
        in_specs=(P("samp", None), P("samp", "reg"), P(None, "reg")),
        out_specs=P(None, "reg"),
        check_vma=False,
    )
```

```python
import jax
import jax.numpy as jnp
from jax import lax
from jax.experimental import pallas as pl
from jax.experimental.pallas import tpu as pltpu
from jax.sharding import PartitionSpec as P

STEP_SCALE = 0.5
PENALTY = 40.0
EPSILON = 1e-06
LANES = 128
F32 = jnp.float32
BF16 = jnp.bfloat16
VMEM_LIMIT = 48 << 20
N_X = 4


def params():
    return pltpu.CompilerParams(vmem_limit_bytes=VMEM_LIMIT)


def to_column(row, first, rows):
    lane = lax.broadcasted_iota(jnp.int32, (rows, LANES), 1)
    own = lax.broadcasted_iota(jnp.int32, (rows, LANES), 0) + first
    return jnp.sum(jnp.where(lane == own, row, 0.0), axis=1, keepdims=True)


def to_row(column):
    rows = column.shape[0]
    lane = lax.broadcasted_iota(jnp.int32, (rows, LANES), 1)
    own = lax.broadcasted_iota(jnp.int32, (rows, LANES), 0)
    return jnp.sum(jnp.where(lane == own, column, 0.0), axis=0, keepdims=True)


def correlate_kernel(place, lib_hbm, resp_hbm, coef_hbm, out, lib, resp, coef, acc, squares, sems, *, blocks, chunks):
    count = len(blocks)
    starts = [sum(blocks[:i]) for i in range(count)]
    unit = blocks[0]

    def rows_copy(source, target, at, size, sem):
        return pltpu.make_async_copy(source.at[pl.ds(at, size)], target.at[pl.ds(at, size)], sems.at[sem])

    copy_coef = pltpu.make_async_copy(coef_hbm, coef, sems.at[0])
    copies = []
    slot = 1
    for at, size in zip(starts, blocks):
        own = [rows_copy(lib_hbm, lib, at + j * unit, unit, slot + j) for j in range(size // unit)]
        own.append(rows_copy(resp_hbm, resp, at, size, slot + len(own)))
        slot += len(own)
        copies.append(own)
    copy_coef.start()
    for own in copies:
        for copy in own:
            copy.start()
    copy_coef.wait()
    weights = coef[...].astype(BF16)
    columns = pl.multiple_of(place[1] * LANES, LANES)
    residuals = {}

    def residual(i):
        for copy in copies[i]:
            copy.wait()
        at = pl.ds(starts[i], blocks[i])
        fit = jnp.dot(lib[at, :], weights, preferred_element_type=F32)
        residuals[i] = (fit - resp[at, :].astype(F32)).astype(BF16)

    def correlation(i):
        at = pl.ds(starts[i], blocks[i])
        block = lib[at, :]
        right = jnp.concatenate([residuals[i], lib[at, pl.ds(columns, LANES)]], axis=1)
        part = lax.dot_general(block, right, (((0,), (0,)), ((), ())), preferred_element_type=F32)
        wide = block.astype(F32)
        part_sq = jnp.sum((wide * wide).reshape(-1, 8, wide.shape[1]), axis=0)
        if i == 0:
            acc[...] = part
            squares[...] = part_sq
        else:
            acc[...] += part
            squares[...] += part_sq

    for i in range(count):
        residual(i)
        if i > 0:
            correlation(i - 1)
    correlation(count - 1)

    rows = acc.shape[0] // chunks
    tall = 2 * rows + 1
    column_sq = jnp.sum(squares[...], axis=0, keepdims=True)
    for c in range(chunks):
        out[c * tall:c * tall + rows, :] = acc[c * rows:(c + 1) * rows, :LANES]
        out[c * tall + rows:c * tall + 2 * rows, :] = acc[c * rows:(c + 1) * rows, LANES:]
        at = c * rows // LANES * LANES
        out[c * tall + 2 * rows:(c + 1) * tall, :] = column_sq[:, at:at + LANES]


def block_sizes(samples):
    unit = samples // 12
    return (unit, 2 * unit, 3 * unit, 3 * unit, 3 * unit)


def correlate(place, library, responses, coefficients, chunks):
    samples, terms = library.shape
    blocks = block_sizes(samples)
    hbm = pl.BlockSpec(memory_space=pltpu.HBM)
    return pl.pallas_call(
        lambda *refs: correlate_kernel(*refs, blocks=blocks, chunks=chunks),
        out_shape=jax.ShapeDtypeStruct((2 * terms + chunks, LANES), F32),
        in_specs=[pl.BlockSpec(memory_space=pltpu.SMEM), hbm, hbm, hbm],
        scratch_shapes=[
            pltpu.VMEM((samples, terms), BF16),
            pltpu.VMEM((samples, LANES), BF16),
            pltpu.VMEM((terms, LANES), F32),
            pltpu.VMEM((terms, 2 * LANES), F32),
            pltpu.VMEM((8, terms), F32),
            pltpu.SemaphoreType.DMA((1 + samples // blocks[0] + len(blocks),)),
        ],
        compiler_params=params(),
        name="correlate",
    )(place, library, *(pltpu.with_memory_space_constraint(a, pltpu.HBM) for a in (responses, coefficients)))


def add_kernel(parts, out):
    tall = out.shape[0]
    total = parts[0:tall, :]
    for c in range(1, parts.shape[0] // tall):
        total += parts[c * tall:(c + 1) * tall, :]
    out[...] = total


def first_step_kernel(place, parts, coef, send, state, *, rows, samples):
    tall = 2 * rows + 1
    total = parts[0:2 * rows, :]
    column_sq = parts[2 * rows:tall, :]
    for c in range(1, parts.shape[0] // tall):
        total += parts[c * tall:c * tall + 2 * rows, :]
        column_sq += parts[c * tall + 2 * rows:(c + 1) * tall, :]
    step = STEP_SCALE * samples / to_column(column_sq, place[0] * rows % LANES, rows)
    corr, gram = total[:rows], total[rows:]
    trial = coef[...] - step * (corr / samples)
    squares = to_row(jnp.sum(trial * trial, axis=1, keepdims=True))
    for c in range(8):
        send[c * (rows + 1):c * (rows + 1) + rows, :] = gram
        send[c * (rows + 1) + rows:(c + 1) * (rows + 1), :] = squares
    state[0:rows, :] = trial
    state[rows:2 * rows, :] = corr
    state[2 * rows:3 * rows, :] = jnp.broadcast_to(step, (rows, LANES))


def shrink(trial, squares, step):
    norms = jnp.sqrt(squares + EPSILON)
    return trial * jnp.maximum(0.0, 1.0 - PENALTY * step / norms)


def first_shrink_kernel(gathered, state, moved, own_out, *, rows):
    squares = gathered[rows:rows + 1, :]
    for c in range(1, 8):
        squares += gathered[c * (rows + 1) + rows:(c + 1) * (rows + 1), :]
    own = shrink(state[0:rows, :], to_column(squares, 0, rows), state[2 * rows:3 * rows, :])
    own_out[...] = own
    for c in range(32):
        moved[c * rows:(c + 1) * rows, :] = own


def second_step_kernel(moved, coef, gathered, state, own, send, trial_out, *, rows, samples):
    change = moved[...].astype(BF16).astype(F32) - coef[...].astype(BF16).astype(F32)
    corr = state[rows:2 * rows, :]
    for c in range(8):
        corr += jnp.dot(
            gathered[c * (rows + 1):c * (rows + 1) + rows, :],
            change[c * LANES:(c + 1) * LANES, :],
            precision=lax.Precision.HIGHEST,
            preferred_element_type=F32,
        )
    trial = own[...] - state[2 * rows:3 * rows, :] * (corr / samples)
    squares = to_row(jnp.sum(trial * trial, axis=1, keepdims=True))
    send[...] = jnp.broadcast_to(squares, (8, LANES))
    trial_out[...] = trial


def second_shrink_kernel(squares, trial, state, moved, *, rows):
    total = jnp.sum(squares[...], axis=0, keepdims=True)
    own = shrink(trial[...], to_column(total, 0, rows), state[2 * rows:3 * rows, :])
    for c in range(32):
        moved[c * rows:(c + 1) * rows, :] = own


def whole(kernel, name, out_shapes, *arrays, **fixed):
    return pl.pallas_call(
        lambda *refs: kernel(*refs, **fixed),
        out_shape=[jax.ShapeDtypeStruct(s, F32) for s in out_shapes],
        compiler_params=params(),
        name=name,
    )(*arrays)


def exchange(array, axis, count, groups=None):
    blocks = array.reshape(count, array.shape[0] // count, 1, LANES)
    return lax.all_to_all(blocks, axis, 0, 0, axis_index_groups=groups).reshape(array.shape)


def shards(library, responses, coefficients):
    n_samp, n_reg = lax.axis_size("samp"), lax.axis_size("reg")
    samples, terms = library.shape[0] * n_samp, library.shape[1]
    rows = terms // n_samp
    place = jnp.stack([lax.axis_index("samp"), lax.axis_index("reg")]).astype(jnp.int32)

    n_z = n_samp // N_X
    over_x = [[x * n_z + z for x in range(N_X)] for z in range(n_z)]
    over_z = [[x * n_z + z for z in range(n_z)] for x in range(N_X)]
    parts = correlate(place, library, responses, coefficients, n_samp)
    parts = exchange(parts, "samp", N_X, over_x)
    (parts,) = whole(add_kernel, "add", [(parts.shape[0] // N_X, LANES)], parts)
    parts = exchange(parts, "samp", n_z, over_z)

    send, state = pl.pallas_call(
        lambda *refs: first_step_kernel(*refs, rows=rows, samples=samples),
        out_shape=[
            jax.ShapeDtypeStruct((n_reg * (rows + 1), LANES), F32),
            jax.ShapeDtypeStruct((3 * rows, LANES), F32),
        ],
        grid_spec=pltpu.PrefetchScalarGridSpec(
            num_scalar_prefetch=1,
            grid=(1,),
            in_specs=[
                pl.BlockSpec(parts.shape, lambda i, place: (0, 0)),
                pl.BlockSpec((rows, LANES), lambda i, place: (place[0], 0)),
            ],
            out_specs=[
                pl.BlockSpec((n_reg * (rows + 1), LANES), lambda i, place: (0, 0)),
                pl.BlockSpec((3 * rows, LANES), lambda i, place: (0, 0)),
            ],
        ),
        compiler_params=params(),
        name="first_step",
    )(place, parts, coefficients)
    gathered = exchange(send, "reg", n_reg)

    spread, own = whole(
        first_shrink_kernel, "first_shrink", [(terms, LANES), (rows, LANES)], gathered, state, rows=rows
    )
    moved = exchange(spread, "samp", n_samp)

    send, trial = whole(
        second_step_kernel, "second_step", [(n_reg, LANES), (rows, LANES)],
        moved, coefficients, gathered, state, own, rows=rows, samples=samples,
    )
    squares = exchange(send, "reg", n_reg)
    (spread,) = whole(
        second_shrink_kernel, "second_shrink", [(terms, LANES)], squares, trial, state, rows=rows
    )
    return exchange(spread, "samp", n_samp)


def solution(mesh):
    return jax.shard_map(
        shards,
        mesh=mesh,
        in_specs=(P("samp", None), P("samp", "reg"), P(None, "reg")),
        out_specs=P(None, "reg"),
        check_vma=False,
    )
```

```python
import jax
import jax.numpy as jnp
from jax import lax
from jax.experimental import pallas as pl
from jax.experimental.pallas import tpu as pltpu
from jax.sharding import PartitionSpec as P

STEP_SCALE = 0.5
PENALTY = 40.0
EPSILON = 1e-06
LANES = 128
F32 = jnp.float32
BF16 = jnp.bfloat16
VMEM_LIMIT = 48 << 20
N_X = 4


def params():
    return pltpu.CompilerParams(vmem_limit_bytes=VMEM_LIMIT)


def to_column(row, rows, first=0, run=None):
    lane = lax.broadcasted_iota(jnp.int32, (rows, LANES), 1)
    own = lax.broadcasted_iota(jnp.int32, (rows, LANES), 0)
    if run is not None:
        own = jnp.where(own < run, own, own - run + LANES // 2)
        own = jnp.bitwise_and(own + first, LANES - 1)
    return jnp.sum(jnp.where(lane == own, row, 0.0), axis=1, keepdims=True)


def to_row(column):
    rows = column.shape[0]
    lane = lax.broadcasted_iota(jnp.int32, (rows, LANES), 1)
    own = lax.broadcasted_iota(jnp.int32, (rows, LANES), 0)
    return jnp.sum(jnp.where(lane == own, column, 0.0), axis=0, keepdims=True)


def correlate_kernel(place, lib_hbm, resp_hbm, coef_hbm, out, lib, resp, coef, acc, squares, sems, *, blocks, n_x, n_z):
    count = len(blocks)
    starts = [sum(blocks[:i]) for i in range(count)]
    unit = blocks[0]

    def rows_copy(source, target, at, size, sem):
        return pltpu.make_async_copy(source.at[pl.ds(at, size)], target.at[pl.ds(at, size)], sems.at[sem])

    copy_coef = pltpu.make_async_copy(coef_hbm, coef, sems.at[0])
    copies = []
    slot = 1
    for at, size in zip(starts, blocks):
        own = [rows_copy(lib_hbm, lib, at + j * unit, unit, slot + j) for j in range(size // unit)]
        own.append(rows_copy(resp_hbm, resp, at, size, slot + len(own)))
        slot += len(own)
        copies.append(own)
    copy_coef.start()
    for own in copies:
        for copy in own:
            copy.start()
    copy_coef.wait()
    weights = coef[...].astype(BF16)
    columns = pl.multiple_of(place[1] * LANES, LANES)
    residuals = {}

    def residual(i):
        for copy in copies[i]:
            copy.wait()
        at = pl.ds(starts[i], blocks[i])
        fit = jnp.dot(lib[at, :], weights, preferred_element_type=F32)
        residuals[i] = (fit - resp[at, :].astype(F32)).astype(BF16)

    def correlation(i):
        at = pl.ds(starts[i], blocks[i])
        block = lib[at, :]
        right = jnp.concatenate([residuals[i], lib[at, pl.ds(columns, LANES)]], axis=1)
        part = lax.dot_general(block, right, (((0,), (0,)), ((), ())), preferred_element_type=F32)
        wide = block.astype(F32)
        part_sq = jnp.sum((wide * wide).reshape(-1, 8, wide.shape[1]), axis=0)
        if i == 0:
            acc[...] = part
            squares[...] = part_sq
        else:
            acc[...] += part
            squares[...] += part_sq

    for i in range(count):
        residual(i)
        if i > 0:
            correlation(i - 1)
    correlation(count - 1)

    column_sq = jnp.sum(squares[...], axis=0, keepdims=True)
    of_lane = lax.broadcasted_iota(jnp.int32, (1, LANES), 1)
    run = LANES // n_z
    tall = 4 * run + 1
    for x in range(n_x):
        halves = []
        for b in range(2):
            at = (2 * x + b) * LANES
            corr = acc[at:at + LANES, :LANES]
            gram = acc[at:at + LANES, LANES:].T
            halves.append((corr, gram, column_sq[:, at:at + LANES]))
        turned = jnp.concatenate([halves[1][2][:, LANES // 2:], halves[1][2][:, :LANES // 2]], axis=1)
        for z in range(n_z):
            to = (x * n_z + z) * tall
            for part in range(2):
                for b in range(2):
                    out[to:to + run, :] = halves[b][part][z * run:(z + 1) * run]
                    to += run
            mine = (of_lane >= z * run) & (of_lane < (z + 1) * run)
            out[to:to + 1, :] = jnp.where(mine, halves[0][2], turned)


def block_sizes(samples):
    unit = samples // 12
    return (unit, 2 * unit, 3 * unit, 3 * unit, 3 * unit)


def correlate(place, library, responses, coefficients, n_x, n_z):
    samples, terms = library.shape
    blocks = block_sizes(samples)
    hbm = pl.BlockSpec(memory_space=pltpu.HBM)
    return pl.pallas_call(
        lambda *refs: correlate_kernel(*refs, blocks=blocks, n_x=n_x, n_z=n_z),
        out_shape=jax.ShapeDtypeStruct((2 * terms + n_x * n_z, LANES), F32),
        in_specs=[pl.BlockSpec(memory_space=pltpu.SMEM), hbm, hbm, hbm],
        scratch_shapes=[
            pltpu.VMEM((samples, terms), BF16),
            pltpu.VMEM((samples, LANES), BF16),
            pltpu.VMEM((terms, LANES), F32),
            pltpu.VMEM((terms, 2 * LANES), F32),
            pltpu.VMEM((8, terms), F32),
            pltpu.SemaphoreType.DMA((1 + samples // blocks[0] + len(blocks),)),
        ],
        compiler_params=params(),
        name="correlate",
    )(place, library, *(pltpu.with_memory_space_constraint(a, pltpu.HBM) for a in (responses, coefficients)))


def add_kernel(parts, out):
    tall = out.shape[0]
    total = parts[0:tall, :]
    for c in range(1, parts.shape[0] // tall):
        total += parts[c * tall:(c + 1) * tall, :]
    out[...] = total


def first_step_kernel(place, parts, coef, send, state, *, samples, n_z):
    run = LANES // n_z
    rows = 2 * run
    tall = 2 * rows + 1
    total = parts[0:2 * rows, :]
    column_sq = parts[2 * rows:tall, :]
    for c in range(1, n_z):
        total += parts[c * tall:c * tall + 2 * rows, :]
        column_sq += parts[c * tall + 2 * rows:(c + 1) * tall, :]
    first = place[0] % n_z * run
    step = STEP_SCALE * samples / to_column(column_sq, rows, first, run)
    corr, gram = total[:rows], total[rows:]
    at = pl.multiple_of(place[0] // n_z * 2 * LANES + first, run)
    start = jnp.concatenate([coef[pl.ds(at, run), :], coef[pl.ds(at + LANES, run), :]], axis=0)
    trial = start - step * (corr / samples)
    squares = to_row(jnp.sum(trial * trial, axis=1, keepdims=True))
    for c in range(8):
        send[c * (rows + 1):c * (rows + 1) + rows, :] = gram
        send[c * (rows + 1) + rows:(c + 1) * (rows + 1), :] = squares
    state[0:rows, :] = trial
    state[rows:2 * rows, :] = corr
    state[2 * rows:3 * rows, :] = jnp.broadcast_to(step, (rows, LANES))


def shrink(trial, squares, step):
    norms = jnp.sqrt(squares + EPSILON)
    return trial * jnp.maximum(0.0, 1.0 - PENALTY * step / norms)


def first_shrink_kernel(gathered, state, moved, own_out, *, rows):
    squares = gathered[rows:rows + 1, :]
    for c in range(1, 8):
        squares += gathered[c * (rows + 1) + rows:(c + 1) * (rows + 1), :]
    own = shrink(state[0:rows, :], to_column(squares, rows), state[2 * rows:3 * rows, :])
    own_out[...] = own
    for c in range(moved.shape[0] // rows):
        moved[c * rows:(c + 1) * rows, :] = own


def product_kernel(place, moved, coef, gathered, out, *, n_z):
    run = LANES // n_z
    rows = 2 * run
    at = pl.multiple_of(place[0] // n_z * 2 * LANES, LANES)
    total = jnp.zeros((LANES, LANES), F32)
    for b in range(2):
        new = jnp.concatenate(
            [moved[z * rows + b * run:z * rows + (b + 1) * run, :] for z in range(n_z)], axis=0
        )
        old = coef[pl.ds(at + b * LANES, LANES), :]
        change = new.astype(BF16).astype(F32) - old.astype(BF16).astype(F32)
        gram = jnp.concatenate(
            [gathered[r * (rows + 1) + b * run:r * (rows + 1) + (b + 1) * run, :] for r in range(8)], axis=0
        )
        total += jnp.dot(gram, change, precision=lax.Precision.HIGHEST, preferred_element_type=F32)
    out[...] = total


def second_step_kernel(products, state, own, send, trial_out, *, rows, samples):
    corr = state[rows:2 * rows, :]
    for c in range(products.shape[0] // rows):
        corr += products[c * rows:(c + 1) * rows, :]
    trial = own[...] - state[2 * rows:3 * rows, :] * (corr / samples)
    squares = to_row(jnp.sum(trial * trial, axis=1, keepdims=True))
    send[...] = jnp.broadcast_to(squares, send.shape)
    trial_out[...] = trial


def second_shrink_kernel(squares, trial, state, moved, *, rows):
    total = jnp.sum(squares[...], axis=0, keepdims=True)
    own = shrink(trial[...], to_column(total, rows), state[2 * rows:3 * rows, :])
    for c in range(moved.shape[0] // rows):
        moved[c * rows:(c + 1) * rows, :] = own


def whole(kernel, name, out_shapes, *arrays, place=None, **fixed):
    vmem = pl.BlockSpec(memory_space=pltpu.VMEM)
    in_specs = [vmem] * len(arrays)
    if place is not None:
        arrays, in_specs = (place, *arrays), [pl.BlockSpec(memory_space=pltpu.SMEM), *in_specs]
    return pl.pallas_call(
        lambda *refs: kernel(*refs, **fixed),
        out_shape=[jax.ShapeDtypeStruct(s, F32) for s in out_shapes],
        in_specs=in_specs,
        out_specs=[vmem] * len(out_shapes),
        compiler_params=params(),
        name=name,
    )(*arrays)


def exchange(array, axis, count, groups=None):
    blocks = array.reshape(count, array.shape[0] // count, 1, LANES)
    return lax.all_to_all(blocks, axis, 0, 0, axis_index_groups=groups).reshape(array.shape)


def shards(library, responses, coefficients):
    n_samp, n_reg = lax.axis_size("samp"), lax.axis_size("reg")
    samples, terms = library.shape[0] * n_samp, library.shape[1]
    rows = terms // n_samp
    place = jnp.stack([lax.axis_index("samp"), lax.axis_index("reg")]).astype(jnp.int32)
    n_z = n_samp // N_X
    over_x = [[x * n_z + z for x in range(N_X)] for z in range(n_z)]
    over_z = [[x * n_z + z for z in range(n_z)] for x in range(N_X)]

    parts = correlate(place, library, responses, coefficients, N_X, n_z)
    parts = exchange(parts, "samp", N_X, over_x)
    (parts,) = whole(add_kernel, "add", [(parts.shape[0] // N_X, LANES)], parts)
    parts = exchange(parts, "samp", n_z, over_z)

    send, state = whole(
        first_step_kernel, "first_step", [(n_reg * (rows + 1), LANES), (3 * rows, LANES)],
        parts, coefficients, place=place, samples=samples, n_z=n_z,
    )
    gathered = exchange(send, "reg", n_reg)
    spread, own = whole(
        first_shrink_kernel, "first_shrink", [(n_z * rows, LANES), (rows, LANES)], gathered, state, rows=rows
    )
    moved = exchange(spread, "samp", n_z, over_z)

    (products,) = whole(
        product_kernel, "product", [(LANES, LANES)], moved, coefficients, gathered, place=place, n_z=n_z
    )
    products = exchange(products, "samp", N_X, over_x)
    send, trial = whole(
        second_step_kernel, "second_step", [(n_reg, LANES), (rows, LANES)],
        products, state, own, rows=rows, samples=samples,
    )
    squares = exchange(send, "reg", n_reg)
    (spread,) = whole(
        second_shrink_kernel, "second_shrink", [(terms, LANES)], squares, trial, state, rows=rows
    )
    moved = exchange(spread, "samp", n_samp)
    moved = moved.reshape(N_X, n_z, 2, rows // 2, LANES).transpose(0, 2, 1, 3, 4)
    return moved.reshape(terms, LANES)


def solution(mesh):
    return jax.shard_map(
        shards,
        mesh=mesh,
        in_specs=(P("samp", None), P("samp", "reg"), P(None, "reg")),
        out_specs=P(None, "reg"),
        check_vma=False,
    )
```

```python
import jax
import jax.numpy as jnp
from jax import lax
from jax.experimental import pallas as pl
from jax.experimental.pallas import tpu as pltpu
from jax.sharding import PartitionSpec as P

STEP_SCALE = 0.5
PENALTY = 40.0
EPSILON = 1e-06
LANES = 128
F32 = jnp.float32
BF16 = jnp.bfloat16
VMEM_LIMIT = 48 << 20
N_X = 4


def params():
    return pltpu.CompilerParams(vmem_limit_bytes=VMEM_LIMIT)


def to_column(row, rows, first=0, run=None):
    lane = lax.broadcasted_iota(jnp.int32, (rows, LANES), 1)
    own = lax.broadcasted_iota(jnp.int32, (rows, LANES), 0)
    if run is not None:
        own = jnp.where(own < run, own, own - run + LANES // 2)
        own = jnp.bitwise_and(own + first, LANES - 1)
    return jnp.sum(jnp.where(lane == own, row, 0.0), axis=1, keepdims=True)


def to_row(column):
    rows = column.shape[0]
    lane = lax.broadcasted_iota(jnp.int32, (rows, LANES), 1)
    own = lax.broadcasted_iota(jnp.int32, (rows, LANES), 0)
    return jnp.sum(jnp.where(lane == own, column, 0.0), axis=0, keepdims=True)


def correlate_kernel(lib_hbm, resp_hbm, coef_hbm, out, lib, resp, coef, acc, squares, sems, *, blocks, n_x, n_z):
    count = len(blocks)
    starts = [sum(blocks[:i]) for i in range(count)]
    unit = blocks[0]

    def rows_copy(source, target, at, size, sem):
        return pltpu.make_async_copy(source.at[pl.ds(at, size)], target.at[pl.ds(at, size)], sems.at[sem])

    copy_coef = pltpu.make_async_copy(coef_hbm, coef, sems.at[0])
    copies = []
    slot = 1
    for at, size in zip(starts, blocks):
        own = [rows_copy(lib_hbm, lib, at + j * unit, unit, slot + j) for j in range(size // unit)]
        own.append(rows_copy(resp_hbm, resp, at, size, slot + len(own)))
        slot += len(own)
        copies.append(own)
    copy_coef.start()
    for own in copies:
        for copy in own:
            copy.start()
    copy_coef.wait()
    weights = coef[...].astype(BF16)
    columns = pl.multiple_of(lax.axis_index("reg") * LANES, LANES)
    residuals = {}

    def residual(i):
        for copy in copies[i]:
            copy.wait()
        at = pl.ds(starts[i], blocks[i])
        fit = jnp.dot(lib[at, :], weights, preferred_element_type=F32)
        residuals[i] = (fit - resp[at, :].astype(F32)).astype(BF16)

    def correlation(i):
        at = pl.ds(starts[i], blocks[i])
        block = lib[at, :]
        right = jnp.concatenate([residuals[i], lib[at, pl.ds(columns, LANES)]], axis=1)
        part = lax.dot_general(block, right, (((0,), (0,)), ((), ())), preferred_element_type=F32)
        wide = block.astype(F32)
        part_sq = jnp.sum((wide * wide).reshape(-1, 8, wide.shape[1]), axis=0)
        if i == 0:
            acc[...] = part
            squares[...] = part_sq
        else:
            acc[...] += part
            squares[...] += part_sq

    for i in range(count):
        residual(i)
        if i > 0:
            correlation(i - 1)
    correlation(count - 1)

    column_sq = jnp.sum(squares[...], axis=0, keepdims=True)
    of_lane = lax.broadcasted_iota(jnp.int32, (1, LANES), 1)
    run = LANES // n_z
    tall = 4 * run + 1
    for x in range(n_x):
        halves = []
        for b in range(2):
            at = (2 * x + b) * LANES
            corr = acc[at:at + LANES, :LANES]
            gram = acc[at:at + LANES, LANES:].T
            halves.append((corr, gram, column_sq[:, at:at + LANES]))
        turned = jnp.concatenate([halves[1][2][:, LANES // 2:], halves[1][2][:, :LANES // 2]], axis=1)
        for z in range(n_z):
            to = (x * n_z + z) * tall
            for part in range(2):
                for b in range(2):
                    out[to:to + run, :] = halves[b][part][z * run:(z + 1) * run]
                    to += run
            mine = (of_lane >= z * run) & (of_lane < (z + 1) * run)
            out[to:to + 1, :] = jnp.where(mine, halves[0][2], turned)


def block_sizes(samples):
    unit = samples // 12
    return (unit, 2 * unit, 3 * unit, 3 * unit, 3 * unit)


def correlate(library, responses, coefficients, n_x, n_z):
    samples, terms = library.shape
    blocks = block_sizes(samples)
    hbm = pl.BlockSpec(memory_space=pltpu.HBM)
    return pl.pallas_call(
        lambda *refs: correlate_kernel(*refs, blocks=blocks, n_x=n_x, n_z=n_z),
        out_shape=jax.ShapeDtypeStruct((2 * terms + n_x * n_z, LANES), F32),
        in_specs=[hbm, hbm, hbm],
        scratch_shapes=[
            pltpu.VMEM((samples, terms), BF16),
            pltpu.VMEM((samples, LANES), BF16),
            pltpu.VMEM((terms, LANES), F32),
            pltpu.VMEM((terms, 2 * LANES), F32),
            pltpu.VMEM((8, terms), F32),
            pltpu.SemaphoreType.DMA((1 + samples // blocks[0] + len(blocks),)),
        ],
        compiler_params=params(),
        name="correlate",
    )(library, *(pltpu.with_memory_space_constraint(a, pltpu.HBM) for a in (responses, coefficients)))


def add_kernel(parts, out):
    tall = out.shape[0]
    total = parts[0:tall, :]
    for c in range(1, parts.shape[0] // tall):
        total += parts[c * tall:(c + 1) * tall, :]
    out[...] = total


def first_step_kernel(parts, coef, send, state, *, samples, n_z):
    run = LANES // n_z
    rows = 2 * run
    tall = 2 * rows + 1
    total = parts[0:2 * rows, :]
    column_sq = parts[2 * rows:tall, :]
    for c in range(1, n_z):
        total += parts[c * tall:c * tall + 2 * rows, :]
        column_sq += parts[c * tall + 2 * rows:(c + 1) * tall, :]
    samp = lax.axis_index("samp")
    first = samp % n_z * run
    step = STEP_SCALE * samples / to_column(column_sq, rows, first, run)
    corr, gram = total[:rows], total[rows:]
    at = pl.multiple_of(samp // n_z * 2 * LANES + first, run)
    start = jnp.concatenate([coef[pl.ds(at, run), :], coef[pl.ds(at + LANES, run), :]], axis=0)
    trial = start - step * (corr / samples)
    squares = to_row(jnp.sum(trial * trial, axis=1, keepdims=True))
    for c in range(8):
        send[c * (rows + 1):c * (rows + 1) + rows, :] = gram
        send[c * (rows + 1) + rows:(c + 1) * (rows + 1), :] = squares
    state[0:rows, :] = trial
    state[rows:2 * rows, :] = corr
    state[2 * rows:3 * rows, :] = jnp.broadcast_to(step, (rows, LANES))


def shrink(trial, squares, step):
    norms = jnp.sqrt(squares + EPSILON)
    return trial * jnp.maximum(0.0, 1.0 - PENALTY * step / norms)


def first_shrink_kernel(gathered, state, moved, own_out, *, rows):
    squares = gathered[rows:rows + 1, :]
    for c in range(1, 8):
        squares += gathered[c * (rows + 1) + rows:(c + 1) * (rows + 1), :]
    own = shrink(state[0:rows, :], to_column(squares, rows), state[2 * rows:3 * rows, :])
    own_out[...] = own
    for c in range(moved.shape[0] // rows):
        moved[c * rows:(c + 1) * rows, :] = own


def product_kernel(moved, coef, gathered, out, *, n_z):
    run = LANES // n_z
    rows = 2 * run
    at = pl.multiple_of(lax.axis_index("samp") // n_z * 2 * LANES, 2 * LANES)
    new, gram = [], []
    for b in range(2):
        new += [moved[z * rows + b * run:z * rows + (b + 1) * run, :] for z in range(n_z)]
        gram.append(jnp.concatenate(
            [gathered[r * (rows + 1) + b * run:r * (rows + 1) + (b + 1) * run, :] for r in range(8)], axis=0
        ))
    new = jnp.concatenate(new, axis=0).astype(BF16)
    old = coef[pl.ds(at, 2 * LANES), :].astype(BF16)
    both = jnp.concatenate([new, old], axis=1)
    rest = jnp.concatenate(gram, axis=1)
    total = jnp.zeros((LANES, 2 * LANES), F32)
    for _ in range(3):
        part = rest.astype(BF16)
        rest = rest - part.astype(F32)
        total += jnp.dot(part, both, preferred_element_type=F32)
    out[...] = total[:, :LANES] - total[:, LANES:]


def second_step_kernel(products, state, own, send, trial_out, *, rows, samples):
    corr = state[rows:2 * rows, :]
    for c in range(products.shape[0] // rows):
        corr += products[c * rows:(c + 1) * rows, :]
    trial = own[...] - state[2 * rows:3 * rows, :] * (corr / samples)
    squares = to_row(jnp.sum(trial * trial, axis=1, keepdims=True))
    send[...] = jnp.broadcast_to(squares, send.shape)
    trial_out[...] = trial


def second_shrink_kernel(squares, trial, state, moved, *, rows):
    total = jnp.sum(squares[...], axis=0, keepdims=True)
    own = shrink(trial[...], to_column(total, rows), state[2 * rows:3 * rows, :])
    for c in range(moved.shape[0] // rows):
        moved[c * rows:(c + 1) * rows, :] = own


def whole(kernel, name, out_shapes, *arrays, **fixed):
    vmem = pl.BlockSpec(memory_space=pltpu.VMEM)
    return pl.pallas_call(
        lambda *refs: kernel(*refs, **fixed),
        out_shape=[jax.ShapeDtypeStruct(s, F32) for s in out_shapes],
        in_specs=[vmem] * len(arrays),
        out_specs=[vmem] * len(out_shapes),
        compiler_params=params(),
        name=name,
    )(*arrays)


def exchange(array, axis, count, groups=None):
    blocks = array.reshape(count, array.shape[0] // count, 1, LANES)
    return lax.all_to_all(blocks, axis, 0, 0, axis_index_groups=groups).reshape(array.shape)


def shards(library, responses, coefficients):
    n_samp, n_reg = lax.axis_size("samp"), lax.axis_size("reg")
    samples, terms = library.shape[0] * n_samp, library.shape[1]
    rows = terms // n_samp
    n_z = n_samp // N_X
    over_x = [[x * n_z + z for x in range(N_X)] for z in range(n_z)]
    over_z = [[x * n_z + z for z in range(n_z)] for x in range(N_X)]

    parts = correlate(library, responses, coefficients, N_X, n_z)
    parts = exchange(parts, "samp", N_X, over_x)
    (parts,) = whole(add_kernel, "add", [(parts.shape[0] // N_X, LANES)], parts)
    parts = exchange(parts, "samp", n_z, over_z)

    send, state = whole(
        first_step_kernel, "first_step", [(n_reg * (rows + 1), LANES), (3 * rows, LANES)],
        parts, coefficients, samples=samples, n_z=n_z,
    )
    gathered = exchange(send, "reg", n_reg)
    spread, own = whole(
        first_shrink_kernel, "first_shrink", [(n_z * rows, LANES), (rows, LANES)], gathered, state, rows=rows
    )
    moved = exchange(spread, "samp", n_z, over_z)

    (products,) = whole(
        product_kernel, "product", [(LANES, LANES)], moved, coefficients, gathered, n_z=n_z
    )
    products = exchange(products, "samp", N_X, over_x)
    send, trial = whole(
        second_step_kernel, "second_step", [(n_reg, LANES), (rows, LANES)],
        products, state, own, rows=rows, samples=samples,
    )
    squares = exchange(send, "reg", n_reg)
    (spread,) = whole(
        second_shrink_kernel, "second_shrink", [(terms, LANES)], squares, trial, state, rows=rows
    )
    moved = exchange(spread, "samp", n_samp)
    moved = moved.reshape(N_X, n_z, 2, rows // 2, LANES).transpose(0, 2, 1, 3, 4)
    return moved.reshape(terms, LANES)


def solution(mesh):
    return jax.shard_map(
        shards,
        mesh=mesh,
        in_specs=(P("samp", None), P("samp", "reg"), P(None, "reg")),
        out_specs=P(None, "reg"),
        check_vma=False,
    )
```

```python
import jax
import jax.numpy as jnp
from jax import lax
from jax.experimental import pallas as pl
from jax.experimental.pallas import tpu as pltpu
from jax.sharding import PartitionSpec as P

STEP_SCALE = 0.5
PENALTY = 40.0
EPSILON = 1e-06
LANES = 128
F32 = jnp.float32
BF16 = jnp.bfloat16
VMEM_LIMIT = 48 << 20
N_X = 4


def params():
    return pltpu.CompilerParams(vmem_limit_bytes=VMEM_LIMIT)


def to_column(row, rows, first=0, run=None):
    lane = lax.broadcasted_iota(jnp.int32, (rows, LANES), 1)
    own = lax.broadcasted_iota(jnp.int32, (rows, LANES), 0)
    if run is not None:
        own = jnp.where(own < run, own, own - run + LANES // 2)
        own = jnp.bitwise_and(own + first, LANES - 1)
    return jnp.sum(jnp.where(lane == own, row, 0.0), axis=1, keepdims=True)


def to_row(column):
    rows = column.shape[0]
    lane = lax.broadcasted_iota(jnp.int32, (rows, LANES), 1)
    own = lax.broadcasted_iota(jnp.int32, (rows, LANES), 0)
    return jnp.sum(jnp.where(lane == own, column, 0.0), axis=0, keepdims=True)


def correlate_kernel(lib_hbm, resp_hbm, coef_hbm, out, lib, resp, coef, acc, squares, sems, *, blocks, n_x, n_z):
    count = len(blocks)
    starts = [sum(blocks[:i]) for i in range(count)]
    unit = blocks[0]

    def rows_copy(source, target, at, size, sem):
        return pltpu.make_async_copy(source.at[pl.ds(at, size)], target.at[pl.ds(at, size)], sems.at[sem])

    copy_coef = pltpu.make_async_copy(coef_hbm, coef, sems.at[0])
    copies = []
    slot = 1
    for at, size in zip(starts, blocks):
        own = [rows_copy(lib_hbm, lib, at + j * unit, unit, slot + j) for j in range(size // unit)]
        own.append(rows_copy(resp_hbm, resp, at, size, slot + len(own)))
        slot += len(own)
        copies.append(own)
    copy_coef.start()
    for own in copies:
        for copy in own:
            copy.start()
    copy_coef.wait()
    weights = coef[...].astype(BF16)
    columns = pl.multiple_of(lax.axis_index("reg") * LANES, LANES)
    residuals = {}

    def residual(i):
        for copy in copies[i]:
            copy.wait()
        at = pl.ds(starts[i], blocks[i])
        fit = jnp.dot(lib[at, :], weights, preferred_element_type=F32)
        residuals[i] = (fit - resp[at, :].astype(F32)).astype(BF16)

    def correlation(i):
        at = pl.ds(starts[i], blocks[i])
        block = lib[at, :]
        right = jnp.concatenate([residuals[i], lib[at, pl.ds(columns, LANES)]], axis=1)
        part = lax.dot_general(right, block, (((0,), (0,)), ((), ())), preferred_element_type=F32)
        wide = block.astype(F32)
        part_sq = jnp.sum((wide * wide).reshape(-1, 8, wide.shape[1]), axis=0)
        if i == 0:
            acc[...] = part
            squares[...] = part_sq
        else:
            acc[...] += part
            squares[...] += part_sq

    for i in range(count):
        residual(i)
        if i > 0:
            correlation(i - 1)
    correlation(count - 1)

    column_sq = jnp.sum(squares[...], axis=0, keepdims=True)
    of_lane = lax.broadcasted_iota(jnp.int32, (1, LANES), 1)
    run = LANES // n_z
    tall = 4 * run + 1
    for x in range(n_x):
        halves = []
        for b in range(2):
            at = (2 * x + b) * LANES
            corr = acc[:LANES, at:at + LANES].T
            gram = acc[LANES:, at:at + LANES]
            halves.append((corr, gram, column_sq[:, at:at + LANES]))
        turned = jnp.concatenate([halves[1][2][:, LANES // 2:], halves[1][2][:, :LANES // 2]], axis=1)
        for z in range(n_z):
            to = (x * n_z + z) * tall
            for part in range(2):
                for b in range(2):
                    out[to:to + run, :] = halves[b][part][z * run:(z + 1) * run]
                    to += run
            mine = (of_lane >= z * run) & (of_lane < (z + 1) * run)
            out[to:to + 1, :] = jnp.where(mine, halves[0][2], turned)


def block_sizes(samples):
    unit = samples // 12
    return (unit, 2 * unit, 3 * unit, 3 * unit, 3 * unit)


def correlate(library, responses, coefficients, n_x, n_z):
    samples, terms = library.shape
    blocks = block_sizes(samples)
    hbm = pl.BlockSpec(memory_space=pltpu.HBM)
    return pl.pallas_call(
        lambda *refs: correlate_kernel(*refs, blocks=blocks, n_x=n_x, n_z=n_z),
        out_shape=jax.ShapeDtypeStruct((2 * terms + n_x * n_z, LANES), F32),
        in_specs=[hbm, hbm, hbm],
        scratch_shapes=[
            pltpu.VMEM((samples, terms), BF16),
            pltpu.VMEM((samples, LANES), BF16),
            pltpu.VMEM((terms, LANES), F32),
            pltpu.VMEM((2 * LANES, terms), F32),
            pltpu.VMEM((8, terms), F32),
            pltpu.SemaphoreType.DMA((1 + samples // blocks[0] + len(blocks),)),
        ],
        compiler_params=params(),
        name="correlate",
    )(library, *(pltpu.with_memory_space_constraint(a, pltpu.HBM) for a in (responses, coefficients)))


def add_kernel(parts, out):
    tall = out.shape[0]
    total = parts[0:tall, :]
    for c in range(1, parts.shape[0] // tall):
        total += parts[c * tall:(c + 1) * tall, :]
    out[...] = total


def first_step_kernel(parts, coef, send, state, *, samples, n_z):
    run = LANES // n_z
    rows = 2 * run
    tall = 2 * rows + 1
    total = parts[0:2 * rows, :]
    column_sq = parts[2 * rows:tall, :]
    for c in range(1, n_z):
        total += parts[c * tall:c * tall + 2 * rows, :]
        column_sq += parts[c * tall + 2 * rows:(c + 1) * tall, :]
    samp = lax.axis_index("samp")
    first = samp % n_z * run
    step = STEP_SCALE * samples / to_column(column_sq, rows, first, run)
    corr, gram = total[:rows], total[rows:]
    at = pl.multiple_of(samp // n_z * 2 * LANES + first, run)
    start = jnp.concatenate([coef[pl.ds(at, run), :], coef[pl.ds(at + LANES, run), :]], axis=0)
    trial = start - step * (corr / samples)
    squares = to_row(jnp.sum(trial * trial, axis=1, keepdims=True))
    for c in range(8):
        send[c * (rows + 1):c * (rows + 1) + rows, :] = gram
        send[c * (rows + 1) + rows:(c + 1) * (rows + 1), :] = squares
    state[0:rows, :] = trial
    state[rows:2 * rows, :] = corr
    state[2 * rows:3 * rows, :] = jnp.broadcast_to(step, (rows, LANES))


def shrink(trial, squares, step):
    norms = jnp.sqrt(squares + EPSILON)
    return trial * jnp.maximum(0.0, 1.0 - PENALTY * step / norms)


def first_shrink_kernel(gathered, state, moved, own_out, *, rows):
    squares = gathered[rows:rows + 1, :]
    for c in range(1, 8):
        squares += gathered[c * (rows + 1) + rows:(c + 1) * (rows + 1), :]
    own = shrink(state[0:rows, :], to_column(squares, rows), state[2 * rows:3 * rows, :])
    own_out[...] = own
    for c in range(moved.shape[0] // rows):
        moved[c * rows:(c + 1) * rows, :] = own


def product_kernel(moved, coef, gathered, out, *, n_z):
    run = LANES // n_z
    rows = 2 * run
    at = pl.multiple_of(lax.axis_index("samp") // n_z * 2 * LANES, 2 * LANES)
    new, gram = [], []
    for b in range(2):
        new += [moved[z * rows + b * run:z * rows + (b + 1) * run, :] for z in range(n_z)]
        gram.append(jnp.concatenate(
            [gathered[r * (rows + 1) + b * run:r * (rows + 1) + (b + 1) * run, :] for r in range(8)], axis=0
        ))
    new = jnp.concatenate(new, axis=0).astype(BF16)
    old = coef[pl.ds(at, 2 * LANES), :].astype(BF16)
    both = jnp.concatenate([new, old], axis=1)
    rest = jnp.concatenate(gram, axis=1)
    total = jnp.zeros((LANES, 2 * LANES), F32)
    for _ in range(3):
        part = rest.astype(BF16)
        rest = rest - part.astype(F32)
        total += jnp.dot(part, both, preferred_element_type=F32)
    out[...] = total[:, :LANES] - total[:, LANES:]


def second_step_kernel(products, state, own, send, trial_out, *, rows, samples):
    corr = state[rows:2 * rows, :]
    for c in range(products.shape[0] // rows):
        corr += products[c * rows:(c + 1) * rows, :]
    trial = own[...] - state[2 * rows:3 * rows, :] * (corr / samples)
    squares = to_row(jnp.sum(trial * trial, axis=1, keepdims=True))
    send[...] = jnp.broadcast_to(squares, send.shape)
    trial_out[...] = trial


def second_shrink_kernel(squares, trial, state, moved, *, rows):
    total = jnp.sum(squares[...], axis=0, keepdims=True)
    own = shrink(trial[...], to_column(total, rows), state[2 * rows:3 * rows, :])
    for c in range(moved.shape[0] // rows):
        moved[c * rows:(c + 1) * rows, :] = own


def whole(kernel, name, out_shapes, *arrays, **fixed):
    vmem = pl.BlockSpec(memory_space=pltpu.VMEM)
    return pl.pallas_call(
        lambda *refs: kernel(*refs, **fixed),
        out_shape=[jax.ShapeDtypeStruct(s, F32) for s in out_shapes],
        in_specs=[vmem] * len(arrays),
        out_specs=[vmem] * len(out_shapes),
        compiler_params=params(),
        name=name,
    )(*arrays)


def exchange(array, axis, count, groups=None):
    blocks = array.reshape(count, array.shape[0] // count, 1, LANES)
    return lax.all_to_all(blocks, axis, 0, 0, axis_index_groups=groups).reshape(array.shape)


def shards(library, responses, coefficients):
    n_samp, n_reg = lax.axis_size("samp"), lax.axis_size("reg")
    samples, terms = library.shape[0] * n_samp, library.shape[1]
    rows = terms // n_samp
    n_z = n_samp // N_X
    over_x = [[x * n_z + z for x in range(N_X)] for z in range(n_z)]
    over_z = [[x * n_z + z for z in range(n_z)] for x in range(N_X)]

    parts = correlate(library, responses, coefficients, N_X, n_z)
    parts = exchange(parts, "samp", N_X, over_x)
    (parts,) = whole(add_kernel, "add", [(parts.shape[0] // N_X, LANES)], parts)
    parts = exchange(parts, "samp", n_z, over_z)

    send, state = whole(
        first_step_kernel, "first_step", [(n_reg * (rows + 1), LANES), (3 * rows, LANES)],
        parts, coefficients, samples=samples, n_z=n_z,
    )
    gathered = exchange(send, "reg", n_reg)
    spread, own = whole(
        first_shrink_kernel, "first_shrink", [(n_z * rows, LANES), (rows, LANES)], gathered, state, rows=rows
    )
    moved = exchange(spread, "samp", n_z, over_z)

    (products,) = whole(
        product_kernel, "product", [(LANES, LANES)], moved, coefficients, gathered, n_z=n_z
    )
    products = exchange(products, "samp", N_X, over_x)
    send, trial = whole(
        second_step_kernel, "second_step", [(n_reg, LANES), (rows, LANES)],
        products, state, own, rows=rows, samples=samples,
    )
    squares = exchange(send, "reg", n_reg)
    (spread,) = whole(
        second_shrink_kernel, "second_shrink", [(terms, LANES)], squares, trial, state, rows=rows
    )
    moved = exchange(spread, "samp", n_samp)
    moved = moved.reshape(N_X, n_z, 2, rows // 2, LANES).transpose(0, 2, 1, 3, 4)
    return moved.reshape(terms, LANES)


def solution(mesh):
    return jax.shard_map(
        shards,
        mesh=mesh,
        in_specs=(P("samp", None), P("samp", "reg"), P(None, "reg")),
        out_specs=P(None, "reg"),
        check_vma=False,
    )
```
